128 devices in a mesh: inp: 8 (over z_lo, y), chan: 16 (over z_hi, x, core).
Axes of the slice: x: 4, y: 4, z: 4 (z_hi: 2, z_lo: 2; z = z_hi * 2 + z_lo), core: 2. Of those that a mesh axis runs over, the one named last changes fastest.
Arguments:
- voltages: bfloat16 [256, 256, 8192], P('inp', 'chan'), may hold values from -6 to 6
- history: bfloat16 [256, 7, 8192], P('inp'), may hold values from -6 to 6
- taper: float32 [8, 8192], replicated, may hold values from -2 to 2
Outputs:
- visibility: bfloat16 [2, 2048, 256, 256], P(None, ('inp', 'chan'))
The draws below stay inside these ranges and needn't reach their ends.
All inputs are finite; a program needn't handle non-finite values.
Results may differ from the reference program's by a relative error of at most 0.005.
Values may be sent and summed in bfloat16 or wider, within the bound.
A program may use at most 192 MiB of HBM per device.

```python
import math
import jax
import jax.numpy as jnp
from jax import lax

TAPS = 8
BAND = 2048
FRAME = 8192
LOW = 1024
NIN = 256
SPECTRA = 256


def block_scale(key, shape, cuts, least, top_value):
    def one(dim, parts):
        heights = jax.random.uniform(jax.random.fold_in(jax.random.fold_in(key, 6), dim), (parts,), jnp.float32, least / len(cuts), top_value / len(cuts))
        return jnp.repeat(jnp.exp(heights), shape[dim] // parts).reshape((-1,) + (1,) * (len(shape) - dim - 1))

    level = one(*cuts[0])
    for cut in cuts[1:]:
        level = level * one(*cut)
    return level


def noise(rng, extent, deviation, reach, pieces=(), kind=jnp.bfloat16):
    values = deviation * jax.random.normal(rng, extent, jnp.float32)
    if pieces:
        values = values * block_scale(rng, extent, pieces, -0.22, 0.18)
    return jnp.clip(values, -reach, reach).astype(kind)


def setup_inputs(seed: int = 0) -> dict:
    key_of = jax.random.split(jax.random.key(seed), 4)
    voltages = noise(key_of[0], (NIN, SPECTRA, FRAME), 1.0, 6.0, ((0, 8), (1, 16)))
    history = noise(key_of[1], (NIN, TAPS - 1, FRAME), 1.0, 6.0, ((0, 8),))
    taper = noise(key_of[2], (TAPS, FRAME), 0.35, 2.0, (), jnp.float32)
    return {"voltages": voltages, "history": history, "taper": taper}


def reference(voltages, history, taper):
    scale_factor = 1.0 / math.sqrt(FRAME)

    def one_input(pair_rows):
        earlier, current = pair_rows
        extended = jnp.concatenate([earlier, current], axis=0).astype(jnp.float32)
        filtered = jnp.zeros((SPECTRA, FRAME), jnp.float32)
        for offset in range(TAPS):
            filtered = filtered + taper[offset][None, :] * extended[offset:offset + SPECTRA]
        transformed = jnp.fft.rfft(filtered, axis=-1)[:, LOW:LOW + BAND]
        real_part = jnp.real(transformed) * scale_factor
        imag_part = jnp.imag(transformed) * scale_factor
        return jnp.stack([real_part, imag_part]).astype(jnp.bfloat16)
    spectra = lax.map(one_input, (history, voltages))
    width = 128
    count = BAND // width

    def one_block(block_index):
        start = (block_index * width).astype(jnp.int32)
        piece = lax.dynamic_slice_in_dim(spectra, start, width, axis=3).astype(jnp.float32)
        real_part = piece[:, 0]
        imag_part = piece[:, 1]
        vis_real = jnp.einsum('isk,jsk->kij', real_part, real_part) + jnp.einsum('isk,jsk->kij', imag_part, imag_part)
        vis_imag = jnp.einsum('isk,jsk->kij', imag_part, real_part) - jnp.einsum('isk,jsk->kij', real_part, imag_part)
        return (jnp.stack([vis_real, vis_imag]) / SPECTRA).astype(jnp.bfloat16)
    blocks = lax.map(one_block, jnp.arange(count, dtype=jnp.int32))
    return jnp.transpose(blocks, (1, 0, 2, 3, 4)).reshape(2, BAND, NIN, NIN)
```

```python
import functools
import math

import jax
import jax.numpy as jnp
import ml_dtypes
import numpy as np
from jax import lax
from jax.experimental import pallas as pl
from jax.experimental.pallas import tpu as pltpu
from jax.sharding import PartitionSpec as P

FRAME = 8192
LOW = 1024
BAND = 2048
TAPS = 8
RADIX = 32
INNER = FRAME // RADIX
LANES = 128
NIN = 32
SPECTRA = 16
STRIDE = 16
COLS = FRAME // LANES
SLOTS = 4


def second_stage_tables():
    m = np.arange(INNER, dtype=np.int64)
    k1 = LOW // RADIX + np.arange(BAND // RADIX, dtype=np.int64)

    def angles(k0):
        index = (m[None, :] * (k0 + RADIX * k1[:, None])) % FRAME
        angle = index * (2.0 * math.pi / FRAME)
        return np.cos(angle), np.sin(angle)

    table = np.zeros((RADIX // 2, 4, k1.size, 2, INNER))
    for k0 in range(1, RADIX // 2):
        cos, sin = angles(k0)
        table[k0, 0, :, 0], table[k0, 0, :, 1] = cos, sin
        table[k0, 1, :, 0], table[k0, 1, :, 1] = -sin, cos
        cos, sin = angles(RADIX - k0)
        table[k0, 2, :, 0], table[k0, 2, :, 1] = cos, -sin
        table[k0, 3, :, 0], table[k0, 3, :, 1] = -sin, -cos
    cos, sin = angles(0)
    table[0, 0, :, 0], table[0, 1, :, 0] = cos, -sin
    cos, sin = angles(RADIX // 2)
    table[0, 2, :, 1], table[0, 3, :, 1] = cos, -sin
    table = (table / math.sqrt(FRAME)).reshape(RADIX // 2, 4 * k1.size, 2 * INNER)
    table = table.astype(np.float32)
    high = table.astype(ml_dtypes.bfloat16)
    low = (table - high.astype(np.float32)).astype(ml_dtypes.bfloat16)
    return high, low


def real_fft(values):
    n = len(values)
    if n == 2:
        return [values[0] + values[1], values[0] - values[1]], [None, None]
    even_re, even_im = real_fft(values[0::2])
    odd_re, odd_im = real_fft(values[1::2])
    re, im = [None] * (n // 2 + 1), [None] * (n // 2 + 1)
    re[0], re[n // 2] = even_re[0] + odd_re[0], even_re[0] - odd_re[0]
    re[n // 4], im[n // 4] = even_re[n // 4], -odd_re[n // 4]
    for k in range(1, n // 4):
        cos, sin = math.cos(2 * math.pi * k / n), math.sin(2 * math.pi * k / n)
        if 8 * k == n:
            turned_re = (odd_re[k] + odd_im[k]) * cos
            turned_im = (odd_im[k] - odd_re[k]) * cos
        else:
            turned_re = odd_re[k] * cos + odd_im[k] * sin
            turned_im = odd_im[k] * cos - odd_re[k] * sin
        re[k], im[k] = even_re[k] + turned_re, even_im[k] + turned_im
        re[n // 2 - k], im[n // 2 - k] = even_re[k] - turned_re, turned_im - even_im[k]
    return re, im


def spectra_kernel(
    edges, own_hbm, taper, high_hbm, low_hbm, *rest
):
    if edges:
        left_hbm, right_hbm, history_hbm, out, own, left, right, history, *rest = rest
    else:
        out, own, *rest = rest
    high, low, rows, filtered, turned, gathered, sems = rest
    copies = [pltpu.make_async_copy(own_hbm.at[pl.ds(16 * g, 16)], own.at[pl.ds(16 * g, 16)], sems.at[g]) for g in range(2)]
    if edges:
        copies.append(pltpu.make_async_copy(left_hbm, left, sems.at[2]))
        copies.append(pltpu.make_async_copy(right_hbm, right, sems.at[3]))
        copies.append(pltpu.make_async_copy(history_hbm, history, sems.at[4]))
    tables = [pltpu.make_async_copy(high_hbm, high, sems.at[5]), pltpu.make_async_copy(low_hbm, low, sems.at[6])]
    for copy in copies + tables:
        copy.start()
    for copy in copies:
        copy.wait()
    if edges:
        first = lax.axis_index("chan") == 0
        last = lax.axis_index("chan") == lax.axis_size("chan") - 1

    def column(group, col, slot):
        base = slot * 16 * STRIDE
        lanes = pl.ds(pl.multiple_of(col * LANES, LANES), LANES)
        for i in range(16):
            rows[pl.ds(base + i * STRIDE, 16), :] = own[group * 16 + i, :, lanes].astype(jnp.float32)

    def fir(group, col, slot):
        base = slot * 16 * STRIDE
        lanes = pl.ds(pl.multiple_of(col * LANES, LANES), LANES)
        taps = taper[:, lanes]
        taps = [jnp.broadcast_to(taps[t : t + 1], (8, LANES)) for t in range(TAPS)]
        if edges:
            inputs = pl.ds(pl.multiple_of(group * 16, 16), 16)
            past = [history[f, inputs, lanes].astype(jnp.float32) for f in range(7)]
            before = [left[f, inputs, lanes].astype(jnp.float32) for f in range(4)]
            before = [jnp.where(first, past[3 + f], before[f]) for f in range(4)]
            after = [right[f, inputs, lanes].astype(jnp.float32) for f in range(3)]
        for h in range(2):
            def frame(f):
                return rows[pl.ds(base + 8 * h * STRIDE + f, 8, stride=STRIDE), :]

            def half(value):
                return value[8 * h : 8 * h + 8]

            if edges:
                near = [frame(f) for f in range(16) if f != 7]
                start = [half(b) for b in before] + near[:7]
                tail = near[7:]
                end = [jnp.where(last, half(past[f]), tail[1 + f]) for f in range(7)] + [half(a) for a in after]
                windows = [start[o : o + TAPS] for o in range(4)] + [tail] + [end[o : o + TAPS] for o in range(3)]
            else:
                near = [frame(f) for f in range(15)]
                windows = [near[o : o + TAPS] for o in range(8)]
            for o, window in enumerate(windows):
                total = window[0] * taps[0]
                for t in range(1, TAPS):
                    total = total + window[t] * taps[t]
                filtered[o, col, pl.ds(8 * h, 8), :] = total

    def group_step(group, carry):
        def columns(step, carry):
            for slot in range(SLOTS):
                column(group, step * SLOTS + slot, slot)
            for slot in range(SLOTS):
                fir(group, step * SLOTS + slot, slot)
            return carry

        lax.fori_loop(0, COLS // SLOTS, columns, 0)

        def first_stage(o, carry):
            for part in range(2):
                for h in range(2):
                    values = [filtered[o, 2 * a + part, pl.ds(8 * h, 8), :] for a in range(RADIX)]
                    re, im = real_fft(values)
                    im[0] = re[RADIX // 2]
                    row = pl.ds(pl.multiple_of(o * NIN + group * 16 + 8 * h, 8), 8)
                    for k in range(RADIX // 2):
                        turned[2 * k, row, part * LANES : (part + 1) * LANES] = re[k]
                        turned[2 * k + 1, row, part * LANES : (part + 1) * LANES] = im[k]
            return carry

        lax.fori_loop(0, 8, first_stage, 0)
        return carry

    lax.fori_loop(0, 2, group_step, 0)
    for copy in tables:
        copy.wait()

    def second_stage(k, carry):
        both = jnp.concatenate([turned[2 * k], turned[2 * k + 1]], axis=1)
        both_high = both.astype(jnp.bfloat16)
        both_low = (both - both_high.astype(jnp.float32)).astype(jnp.bfloat16)

        def product(table, value):
            return lax.dot_general(table, value, (((1,), (1,)), ((), ())), preferred_element_type=jnp.float32)

        result = product(high[k], both_high) + product(high[k], both_low) + product(low[k], both_high)
        other = lax.rem(RADIX // 2 - k, RADIX // 2)
        for block in range(4):
            begin = 32 * (block // 2) + 16 * (block % 2) + (other if block >= 2 else k)
            for tile in range(2):
                gathered[tile, pl.ds(begin, 64, stride=64), :] = result[
                    64 * block : 64 * block + 64, tile * LANES : (tile + 1) * LANES
                ]
        return carry

    lax.fori_loop(0, RADIX // 2, second_stage, 0)

    def emit(block, carry):
        for tile in range(2):
            value = gathered[tile, pl.ds(pl.multiple_of(block * 256, 256), 256), :].astype(jnp.bfloat16)
            out[pl.ds(block * 8, 8), tile] = value.reshape(8, 32, LANES)
        return carry

    lax.fori_loop(0, 16, emit, 0)


def spectra_half(edges, voltages, taper, high, low, *halo):
    any_space = pl.BlockSpec(memory_space=pl.ANY)
    vmem = pl.BlockSpec(memory_space=pltpu.VMEM)
    scratch = [pltpu.VMEM((NIN, SPECTRA, FRAME), jnp.bfloat16)]
    if edges:
        scratch += [pltpu.VMEM((f, NIN, FRAME), jnp.bfloat16) for f in (4, 3, 7)]
    scratch += [
        pltpu.VMEM((16, 256, 512), jnp.bfloat16),
        pltpu.VMEM((16, 256, 512), jnp.bfloat16),
        pltpu.VMEM((SLOTS * 16 * STRIDE, LANES), jnp.float32),
        pltpu.VMEM((8, COLS, 16, LANES), jnp.float32),
        pltpu.VMEM((RADIX, 256, 256), jnp.float32),
        pltpu.VMEM((2, 4096, LANES), jnp.float32),
        pltpu.SemaphoreType.DMA((7,)),
    ]
    return pl.pallas_call(
        functools.partial(spectra_kernel, edges),
        out_shape=jax.ShapeDtypeStruct((128, 2, 32, LANES), jnp.bfloat16),
        in_specs=[any_space, vmem, any_space, any_space] + [any_space] * len(halo),
        out_specs=vmem,
        scratch_shapes=scratch,
        compiler_params=pltpu.CompilerParams(vmem_limit_bytes=58 << 20),
        cost_estimate=pl.CostEstimate(flops=20_000_000_000, bytes_accessed=20_000_000, transcendentals=0),
        name="spectra_edges" if edges else "spectra_inner",
    )(voltages, taper, high, low, *halo)


def correlate_kernel(first_ref, second_ref, out, rows, matrix):
    @pl.when(pl.program_id(0) == 0)
    def _():
        lane = lax.broadcasted_iota(jnp.int32, (16, LANES), 1)
        lower = lane < 64
        even = lane % 64 < 32
        for which, ref in enumerate((first_ref, second_ref)):
            def regroup(step, carry):
                tile, part, quad = step // 4, (step // 2) % 2, step % 2
                for a in range(4):
                    for src in range(16):
                        value = ref[(quad * 4 + a) * 16 + src, tile, pl.ds(pl.multiple_of(part * 16, 16), 16), :]
                        rows[pl.ds((a * 16 + src) * 16, 16), :] = value.astype(jnp.float32)
                for c in range(16):
                    t = [rows[pl.ds(a * 256 + c, 16, stride=16), :] for a in range(4)]
                    u = [None] * 4
                    for a in range(2):
                        u[a] = jnp.where(lower, t[a], pltpu.roll(t[a + 2], 64, 1))
                        u[a + 2] = jnp.where(lower, pltpu.roll(t[a], 64, 1), t[a + 2])
                    for a in (0, 2):
                        for b, value in enumerate(
                            (
                                jnp.where(even, u[a], pltpu.roll(u[a + 1], 32, 1)),
                                jnp.where(even, pltpu.roll(u[a], 96, 1), u[a + 1]),
                            )
                        ):
                            row = pl.ds(pl.multiple_of(((which * 2 + tile) * 4 + a + b) * 16, 16), 16)
                            lanes = pl.ds(pl.multiple_of(quad * LANES, LANES), LANES)
                            matrix[c, part, row, lanes] = value.astype(jnp.bfloat16)
                return carry

            lax.fori_loop(0, 8, regroup, 0)

    c = pl.program_id(0)
    re, im = matrix[c, 0], matrix[c, 1]

    def product(left, right):
        return lax.dot_general(left, right, (((0,), (0,)), ((), ())), preferred_element_type=jnp.float32)

    scale = 1.0 / 256.0
    out[0, 0] = ((product(re, re) + product(im, im)) * scale).astype(jnp.bfloat16)
    out[1, 0] = ((product(im, re) - product(re, im)) * scale).astype(jnp.bfloat16)


def correlate(first, second):
    shape = first.shape
    whole = pl.BlockSpec(shape, lambda c: (0, 0, 0, 0), pipeline_mode=pl.Buffered(1))
    return pl.pallas_call(
        correlate_kernel,
        grid=(16,),
        out_shape=jax.ShapeDtypeStruct((2, 16, 256, 256), jnp.bfloat16),
        in_specs=[whole, whole],
        out_specs=pl.BlockSpec((2, 1, 256, 256), lambda c: (0, c, 0, 0)),
        scratch_shapes=[pltpu.VMEM((1024, LANES), jnp.float32), pltpu.VMEM((16, 2, 256, 256), jnp.bfloat16)],
        compiler_params=pltpu.CompilerParams(vmem_limit_bytes=40 << 20),
        cost_estimate=pl.CostEstimate(flops=4_300_000_000, bytes_accessed=9_000_000, transcendentals=0),
        name="correlate",
    )(first, second)


def on_device(voltages, history, taper):
    high, low = (jnp.asarray(t) for t in second_stage_tables())
    chan = lax.axis_size("chan")
    left = jnp.transpose(voltages[:, SPECTRA - 4 :], (1, 0, 2))
    right = jnp.transpose(voltages[:, :3], (1, 0, 2))
    left = lax.ppermute(left, "chan", [(i, i + 1) for i in range(chan - 1)])
    right = lax.ppermute(right, "chan", [(i, (i - 1) % chan) for i in range(chan)])
    history = jnp.transpose(history, (1, 0, 2))

    def exchange(value):
        return lax.all_to_all(value, ("inp", "chan"), split_axis=0, concat_axis=0, tiled=True)

    inner = exchange(spectra_half(False, voltages, taper, high, low))
    edge = exchange(spectra_half(True, voltages, taper, high, low, left, right, history))
    return correlate(inner, edge)


def solution(mesh):
    in_specs = (P("inp", "chan", None), P("inp", None, None), P())
    out_specs = P(None, ("inp", "chan"), None, None)
    return jax.shard_map(on_device, mesh=mesh, in_specs=in_specs, out_specs=out_specs, check_vma=False)
```

```python
import functools
import math

import jax
import jax.numpy as jnp
import ml_dtypes
import numpy as np
from jax import lax
from jax.experimental import pallas as pl
from jax.experimental.pallas import tpu as pltpu
from jax.sharding import PartitionSpec as P

FRAME = 8192
LOW = 1024
BAND = 2048
TAPS = 8
RADIX = 32
INNER = FRAME // RADIX
LANES = 128
NIN = 32
SPECTRA = 16
STRIDE = 17
GAP = 65

COLS = FRAME // LANES
SLOTS = 4
PIECES = 4


def second_stage_tables():
    m = np.arange(INNER, dtype=np.int64)
    k1 = LOW // RADIX + np.arange(BAND // RADIX, dtype=np.int64)

    def angles(k0):
        index = (m[None, :] * (k0 + RADIX * k1[:, None])) % FRAME
        angle = index * (2.0 * math.pi / FRAME)
        return np.cos(angle), np.sin(angle)

    table = np.zeros((RADIX // 2, 4, k1.size, 2, INNER))
    for k0 in range(1, RADIX // 2):
        cos, sin = angles(k0)
        table[k0, 0, :, 0], table[k0, 0, :, 1] = cos, sin
        table[k0, 1, :, 0], table[k0, 1, :, 1] = -sin, cos
        cos, sin = angles(RADIX - k0)
        table[k0, 2, :, 0], table[k0, 2, :, 1] = cos, -sin
        table[k0, 3, :, 0], table[k0, 3, :, 1] = -sin, -cos
    cos, sin = angles(0)
    table[0, 0, :, 0], table[0, 1, :, 0] = cos, -sin
    cos, sin = angles(RADIX // 2)
    table[0, 2, :, 1], table[0, 3, :, 1] = cos, -sin
    table = (table / math.sqrt(FRAME)).reshape(RADIX // 2, 4 * k1.size, 2 * INNER)
    table = table.astype(np.float32)
    high = table.astype(ml_dtypes.bfloat16)
    low = (table - high.astype(np.float32)).astype(ml_dtypes.bfloat16)
    return high, low


def real_fft(values):
    n = len(values)
    if n == 2:
        return [values[0] + values[1], values[0] - values[1]], [None, None]
    even_re, even_im = real_fft(values[0::2])
    odd_re, odd_im = real_fft(values[1::2])
    re, im = [None] * (n // 2 + 1), [None] * (n // 2 + 1)
    re[0], re[n // 2] = even_re[0] + odd_re[0], even_re[0] - odd_re[0]
    re[n // 4], im[n // 4] = even_re[n // 4], -odd_re[n // 4]
    for k in range(1, n // 4):
        cos, sin = math.cos(2 * math.pi * k / n), math.sin(2 * math.pi * k / n)
        if 8 * k == n:
            turned_re = (odd_re[k] + odd_im[k]) * cos
            turned_im = (odd_im[k] - odd_re[k]) * cos
        else:
            turned_re = odd_re[k] * cos + odd_im[k] * sin
            turned_im = odd_im[k] * cos - odd_re[k] * sin
        re[k], im[k] = even_re[k] + turned_re, even_im[k] + turned_im
        re[n // 2 - k], im[n // 2 - k] = even_re[k] - turned_re, turned_im - even_im[k]
    return re, im


def regroup(ref, rows, matrix, offset):
    lane = lax.broadcasted_iota(jnp.int32, (16, LANES), 1)
    lower = lane < 64
    even = lane % 64 < 32

    def step(index, carry):
        tile, part, quad = index // 4, (index // 2) % 2, index % 2
        for a in range(4):
            for src in range(16):
                value = ref[(quad * 4 + a) * 16 + src, tile, pl.ds(pl.multiple_of(part * 16, 16), 16), :]
                rows[pl.ds((a * 16 + src) * STRIDE, 16), :] = value.astype(jnp.float32)
        for c in range(16):
            t = [rows[pl.ds(a * 16 * STRIDE + c, 16, stride=STRIDE), :] for a in range(4)]
            u = [None] * 4
            for a in range(2):
                u[a] = jnp.where(lower, t[a], pltpu.roll(t[a + 2], 64, 1))
                u[a + 2] = jnp.where(lower, pltpu.roll(t[a], 64, 1), t[a + 2])
            for a in (0, 2):
                first = jnp.where(even, u[a], pltpu.roll(u[a + 1], 32, 1))
                second = jnp.where(even, pltpu.roll(u[a], 96, 1), u[a + 1])
                for b, value in enumerate((first, second)):
                    row = pl.ds(pl.multiple_of(offset + (tile * 4 + a + b) * 16, 16), 16)
                    lanes = pl.ds(pl.multiple_of(quad * LANES, LANES), LANES)
                    matrix[c, part, row, lanes] = value.astype(jnp.bfloat16)
        return carry

    lax.fori_loop(0, 8, step, 0)


def exchange(send, got, local_sem, send_sem, recv_sem):
    inp, chan = lax.axis_index("inp"), lax.axis_index("chan")
    me = inp * 16 + chan
    x, y, z, core = chan // 2 % 4, inp % 4, chan // 8 * 2 + inp // 4, chan % 2

    def step(n, carry):
        n = n * 37 % 128
        to_x, to_y, to_z = (x + n // 2 % 4) % 4, (y + n // 8 % 4) % 4, (z + n // 32) % 4
        to_inp, to_chan = to_z % 2 * 4 + to_y, to_z // 2 * 8 + to_x * 2 + (core + n) % 2
        pltpu.make_async_remote_copy(
            src_ref=send.at[to_inp * 16 + to_chan],
            dst_ref=got.at[me],
            send_sem=send_sem,
            recv_sem=recv_sem,
            device_id=(to_inp, to_chan),
            device_id_type=pl.DeviceIdType.MESH,
        ).start()
        return carry

    lax.fori_loop(1, 128, step, 0)
    local = pltpu.make_async_copy(send.at[me], got.at[me], local_sem)
    local.start()
    return local


def all_copies(send, got, send_sem, recv_sem):
    return pltpu.make_async_remote_copy(
        src_ref=send.at[pl.ds(0, 127)],
        dst_ref=got.at[pl.ds(0, 127)],
        send_sem=send_sem,
        recv_sem=recv_sem,
        device_id=(lax.axis_index("inp"), lax.axis_index("chan")),
        device_id_type=pl.DeviceIdType.MESH,
    )


def spectra_kernel(
    own_hbm, taper, high_hbm, low_hbm, history_hbm, matrix,
    own, history, left_send, right_send, left, right, high, low, rows, filtered, turned, gathered,
    sends, gots, load_sems, table_sems, halo_send_sems, halo_recv_sems, local_sems, send_sems, recv_sems,
):
    inp, chan = lax.axis_index("inp"), lax.axis_index("chan")
    chans = lax.axis_size("chan")
    first, last = chan == 0, chan == chans - 1
    width = FRAME // PIECES

    def loads(group, piece):
        inputs, lanes = pl.ds(16 * group, 16), pl.ds(width * piece, width)
        return pltpu.make_async_copy(own_hbm.at[inputs, :, lanes], own.at[inputs, :, lanes], load_sems.at[group, piece])

    tables = [
        pltpu.make_async_copy(high_hbm, high, table_sems.at[0]),
        pltpu.make_async_copy(low_hbm, low, table_sems.at[1]),
        pltpu.make_async_copy(history_hbm, history, table_sems.at[2]),
    ]
    for group in range(2):
        for piece in range(PIECES):
            loads(group, piece).start()
    for copy in tables:
        copy.start()

    def halo_copies(group, piece):
        at = (slice(None), pl.ds(16 * group, 16), pl.ds(width * piece, width))
        return [
            pltpu.make_async_remote_copy(
                src_ref=source.at[at],
                dst_ref=target.at[at],
                send_sem=halo_send_sems.at[n, group, piece],
                recv_sem=halo_recv_sems.at[n, group, piece],
                device_id=(inp, (chan + by) % chans),
                device_id_type=pl.DeviceIdType.MESH,
            )
            for n, (source, target, by) in enumerate(((left_send, left, 1), (right_send, right, chans - 1)))
        ]

    def column(group, col, slot):
        base = slot * 16 * STRIDE
        lanes = pl.ds(pl.multiple_of(col * LANES, LANES), LANES)
        for i in range(16):
            rows[pl.ds(base + i * STRIDE, 16), :] = own[group * 16 + i, :, lanes].astype(jnp.float32)

    def fir(edges, group, col, slot):
        base = slot * 16 * STRIDE
        lanes = pl.ds(pl.multiple_of(col * LANES, LANES), LANES)
        taps = taper[:, lanes]
        taps = [jnp.broadcast_to(taps[t : t + 1], (8, LANES)) for t in range(TAPS)]
        inputs = pl.ds(pl.multiple_of(group * 16, 16), 16)
        near = [rows[pl.ds(base + f, 16, stride=STRIDE), :] for f in range(16)]
        if edges:
            past = [history[f, inputs, lanes].astype(jnp.float32) for f in range(7)]
            before = [jnp.where(first, past[3 + f], left[f, inputs, lanes].astype(jnp.float32)) for f in range(4)]
            after = [right[f, inputs, lanes].astype(jnp.float32) for f in range(3)]
            start = before + near[:7]
            end = [jnp.where(last, past[f], near[9 + f]) for f in range(7)] + after
            windows = [start[o : o + TAPS] for o in range(4)] + [near[8:]] + [end[o : o + TAPS] for o in range(3)]
        else:
            for n in range(4):
                left_send[n, inputs, lanes] = near[12 + n].astype(jnp.bfloat16)
            for n in range(3):
                right_send[n, inputs, lanes] = near[n].astype(jnp.bfloat16)
            windows = [near[o : o + TAPS] for o in range(8)]
        for h in range(2):
            for o, window in enumerate(windows):
                total = window[0][8 * h : 8 * h + 8] * taps[0]
                for t in range(1, TAPS):
                    total = total + window[t][8 * h : 8 * h + 8] * taps[t]
                filtered[o, col, pl.ds(8 * h, 8), :] = total

    def half(edges, send):
        for group in range(2):
            def columns(step, carry):
                for slot in range(SLOTS):
                    column(group, step * SLOTS + slot, slot)
                for slot in range(SLOTS):
                    fir(edges, group, step * SLOTS + slot, slot)
                return carry

            for piece in range(PIECES):
                if edges:
                    for copy in halo_copies(group, piece):
                        copy.wait()
                else:
                    loads(group, piece).wait()
                steps = COLS // SLOTS // PIECES
                lax.fori_loop(piece * steps, (piece + 1) * steps, columns, 0)
                if not edges:
                    for copy in halo_copies(group, piece):
                        copy.start()

            def first_stage(o, carry):
                for part in range(2):
                    for h in range(2):
                        values = [filtered[o, 2 * a + part, pl.ds(8 * h, 8), :] for a in range(RADIX)]
                        re, im = real_fft(values)
                        im[0] = re[RADIX // 2]
                        row = pl.ds(pl.multiple_of(o * NIN + group * 16 + 8 * h, 8), 8)
                        for k in range(RADIX // 2):
                            turned[2 * k, row, part * LANES : (part + 1) * LANES] = re[k]
                            turned[2 * k + 1, row, part * LANES : (part + 1) * LANES] = im[k]
                return carry

            lax.fori_loop(0, 8, first_stage, 0)

        if not edges:
            for copy in tables:
                copy.wait()

        def second_stage(k, carry):
            both = jnp.concatenate([turned[2 * k], turned[2 * k + 1]], axis=1)
            both_high = both.astype(jnp.bfloat16)
            both_low = (both - both_high.astype(jnp.float32)).astype(jnp.bfloat16)

            def product(table, value):
                return lax.dot_general(table, value, (((1,), (1,)), ((), ())), preferred_element_type=jnp.float32)

            result = product(high[k], both_high) + product(high[k], both_low) + product(low[k], both_high)
            other = lax.rem(RADIX // 2 - k, RADIX // 2)
            for block in range(4):
                begin = 32 * (block // 2) + 16 * (block % 2) + (other if block >= 2 else k)
                for tile in range(2):
                    gathered[tile, pl.ds(begin, 64, stride=GAP), :] = result[
                        64 * block : 64 * block + 64, tile * LANES : (tile + 1) * LANES
                    ]
            return carry

        lax.fori_loop(0, RADIX // 2, second_stage, 0, unroll=4)

        def emit(block, carry):
            begin = pl.multiple_of(block * 8 * GAP, 8)
            for tile in range(2):
                for h in range(8):
                    value = gathered[tile, pl.ds(begin + h * GAP, 64), :].astype(jnp.bfloat16)
                    send[pl.ds(block * 16 + 2 * h, 2), tile] = value.reshape(2, 32, LANES)
            return carry

        lax.fori_loop(0, 8, emit, 0)

    locals_ = []
    for n in range(2):
        half(n == 1, sends.at[n])
        locals_.append(exchange(sends.at[n], gots.at[n], local_sems.at[n], send_sems.at[n], recv_sems.at[n]))
    for n in range(2):
        copies = all_copies(sends.at[n], gots.at[n], send_sems.at[n], recv_sems.at[n])
        copies.wait_recv()
        locals_[n].wait()
        regroup(gots.at[n], rows, matrix, 128 * n)
    for n in range(2):
        all_copies(sends.at[n], gots.at[n], send_sems.at[n], recv_sems.at[n]).wait_send()


def spectra(voltages, taper, high, low, history):
    any_space = pl.BlockSpec(memory_space=pl.ANY)
    vmem = pl.BlockSpec(memory_space=pltpu.VMEM)
    dma = pltpu.SemaphoreType.DMA
    return pl.pallas_call(
        spectra_kernel,
        out_shape=jax.ShapeDtypeStruct((16, 2, 256, 256), jnp.bfloat16),
        in_specs=[any_space, vmem, any_space, any_space, any_space],
        out_specs=vmem,
        scratch_shapes=[
            pltpu.VMEM((NIN, SPECTRA, FRAME), jnp.bfloat16),
            pltpu.VMEM((7, NIN, FRAME), jnp.bfloat16),
            pltpu.VMEM((4, NIN, FRAME), jnp.bfloat16),
            pltpu.VMEM((3, NIN, FRAME), jnp.bfloat16),
            pltpu.VMEM((4, NIN, FRAME), jnp.bfloat16),
            pltpu.VMEM((3, NIN, FRAME), jnp.bfloat16),
            pltpu.VMEM((16, 256, 512), jnp.bfloat16),
            pltpu.VMEM((16, 256, 512), jnp.bfloat16),
            pltpu.VMEM((SLOTS * 16 * STRIDE, LANES), jnp.float32),
            pltpu.VMEM((8, COLS, 16, LANES), jnp.float32),
            pltpu.VMEM((RADIX, 256, 256), jnp.float32),
            pltpu.VMEM((2, 64 * GAP, LANES), jnp.float32),
            pltpu.VMEM((2, 128, 2, 32, LANES), jnp.bfloat16),
            pltpu.VMEM((2, 128, 2, 32, LANES), jnp.bfloat16),
            dma((2, PIECES)),
            dma((3,)),
            dma((2, 2, PIECES)),
            dma((2, 2, PIECES)),
            dma((2,)),
            dma((2,)),
            dma((2,)),
        ],
        compiler_params=pltpu.CompilerParams(vmem_limit_bytes=60 << 20, has_side_effects=True),
        cost_estimate=pl.CostEstimate(flops=30_000_000_000, bytes_accessed=25_000_000, transcendentals=0),
        name="spectra",
    )(voltages, taper, high, low, history)


def correlate_kernel(matrix, out):
    def product(left, right):
        return lax.dot_general(left, right, (((1,), (0,)), ((), ())), preferred_element_type=jnp.float32)

    scale = 1.0 / 256.0
    for n in range(out.shape[1]):
        re, im = matrix[n, 0], matrix[n, 1]
        re_t, im_t = re.T, im.T
        out[0, n] = ((product(re_t, re) + product(im_t, im)) * scale).astype(jnp.bfloat16)
        out[1, n] = ((product(im_t, re) - product(re_t, im)) * scale).astype(jnp.bfloat16)


def correlate(matrix):
    return pl.pallas_call(
        correlate_kernel,
        grid=(4,),
        out_shape=jax.ShapeDtypeStruct((2, 16, 256, 256), jnp.bfloat16),
        in_specs=[pl.BlockSpec((4, 2, 256, 256), lambda c: (c, 0, 0, 0))],
        out_specs=pl.BlockSpec((2, 4, 256, 256), lambda c: (0, c, 0, 0)),
        compiler_params=pltpu.CompilerParams(vmem_limit_bytes=32 << 20),
        cost_estimate=pl.CostEstimate(flops=4_300_000_000, bytes_accessed=9_000_000, transcendentals=0),
        name="correlate",
    )(matrix)


def on_device(voltages, history, taper):
    high, low = (jnp.asarray(t) for t in second_stage_tables())
    return correlate(spectra(voltages, taper, high, low, jnp.transpose(history, (1, 0, 2))))


def solution(mesh):
    in_specs = (P("inp", "chan", None), P("inp", None, None), P())
    out_specs = P(None, ("inp", "chan"), None, None)
    return jax.shard_map(on_device, mesh=mesh, in_specs=in_specs, out_specs=out_specs, check_vma=False)
```

```python
import functools
import math

import jax
import jax.numpy as jnp
import ml_dtypes
import numpy as np
from jax import lax
from jax.experimental import pallas as pl
from jax.experimental.pallas import tpu as pltpu
from jax.sharding import PartitionSpec as P

FRAME = 8192
LOW = 1024
BAND = 2048
TAPS = 8
RADIX = 32
INNER = FRAME // RADIX
LANES = 128
NIN = 32
SPECTRA = 16
STRIDE = 17
GAP = 65

COLS = FRAME // LANES
SLOTS = 4
PIECES = 4


def second_stage_tables():
    m = np.arange(INNER, dtype=np.int64)
    k1 = LOW // RADIX + np.arange(BAND // RADIX, dtype=np.int64)

    def angles(k0):
        index = (m[None, :] * (k0 + RADIX * k1[:, None])) % FRAME
        angle = index * (2.0 * math.pi / FRAME)
        return np.cos(angle), np.sin(angle)

    table = np.zeros((RADIX // 2, 4, k1.size, 2, INNER))
    for k0 in range(1, RADIX // 2):
        cos, sin = angles(k0)
        table[k0, 0, :, 0], table[k0, 0, :, 1] = cos, sin
        table[k0, 1, :, 0], table[k0, 1, :, 1] = -sin, cos
        cos, sin = angles(RADIX - k0)
        table[k0, 2, :, 0], table[k0, 2, :, 1] = cos, -sin
        table[k0, 3, :, 0], table[k0, 3, :, 1] = -sin, -cos
    cos, sin = angles(0)
    table[0, 0, :, 0], table[0, 1, :, 0] = cos, -sin
    cos, sin = angles(RADIX // 2)
    table[0, 2, :, 1], table[0, 3, :, 1] = cos, -sin
    table = (table / math.sqrt(FRAME)).reshape(RADIX // 2, 4 * k1.size, 2 * INNER)
    table = table.astype(np.float32)
    high = table.astype(ml_dtypes.bfloat16)
    low = (table - high.astype(np.float32)).astype(ml_dtypes.bfloat16)
    return high, low


def real_fft(values):
    n = len(values)
    if n == 2:
        return [values[0] + values[1], values[0] - values[1]], [None, None]
    even_re, even_im = real_fft(values[0::2])
    odd_re, odd_im = real_fft(values[1::2])
    re, im = [None] * (n // 2 + 1), [None] * (n // 2 + 1)
    re[0], re[n // 2] = even_re[0] + odd_re[0], even_re[0] - odd_re[0]
    re[n // 4], im[n // 4] = even_re[n // 4], -odd_re[n // 4]
    for k in range(1, n // 4):
        cos, sin = math.cos(2 * math.pi * k / n), math.sin(2 * math.pi * k / n)
        if 8 * k == n:
            turned_re = (odd_re[k] + odd_im[k]) * cos
            turned_im = (odd_im[k] - odd_re[k]) * cos
        else:
            turned_re = odd_re[k] * cos + odd_im[k] * sin
            turned_im = odd_im[k] * cos - odd_re[k] * sin
        re[k], im[k] = even_re[k] + turned_re, even_im[k] + turned_im
        re[n // 2 - k], im[n // 2 - k] = even_re[k] - turned_re, turned_im - even_im[k]
    return re, im


def regroup(ref, rows, matrix, tile, offset, turn):
    lane = lax.broadcasted_iota(jnp.int32, (16, LANES), 1)
    lower = lane < 64
    even = lane % 64 < 32
    ahead = lane % 32 >= 16

    def step(index, carry):
        part, quad = index // 2, index % 2
        for a in range(4):
            for src in range(16):
                value = ref[(quad * 4 + a) * 16 + src, tile, pl.ds(pl.multiple_of(part * 16, 16), 16), :]
                rows[pl.ds((a * 16 + src) * STRIDE, 16), :] = value.astype(jnp.float32)
        for c in range(16):
            t = [rows[pl.ds(a * 16 * STRIDE + c, 16, stride=STRIDE), :] for a in range(4)]
            u = [None] * 4
            for a in range(2):
                u[a] = jnp.where(lower, t[a], pltpu.roll(t[a + 2], 64, 1))
                u[a + 2] = jnp.where(lower, pltpu.roll(t[a], 64, 1), t[a + 2])
            for a in (0, 2):
                first = jnp.where(even, u[a], pltpu.roll(u[a + 1], 32, 1))
                second = jnp.where(even, pltpu.roll(u[a], 96, 1), u[a + 1])
                if turn and a == 0:
                    first = jnp.where(ahead, pltpu.roll(first, 1, 0), first)
                for b, value in enumerate((first, second)):
                    lanes = pl.ds(pl.multiple_of(quad * LANES, LANES), LANES)
                    matrix[c, part, pl.ds(offset + (a + b) * 16, 16), lanes] = value.astype(jnp.bfloat16)
        return carry

    lax.fori_loop(0, 4, step, 0)


def place():
    inp, chan = lax.axis_index("inp"), lax.axis_index("chan")
    x, y, z, core = chan // 2 % 4, inp % 4, chan // 8 * 2 + inp // 4, chan % 2

    def device(n):
        n = n * 37 % 128
        to_x, to_y, to_z = (x + n // 2 % 4) % 4, (y + n // 8 % 4) % 4, (z + n // 32) % 4
        return to_z % 2 * 4 + to_y, to_z // 2 * 8 + to_x * 2 + (core + n) % 2

    return inp, chan, device


def exchange(send, got, tiles, local_sem, send_sem, recv_sem):
    inp, chan, device = place()
    me = inp * 16 + chan

    def step(n, carry):
        to_inp, to_chan = device(n)
        pltpu.make_async_remote_copy(
            src_ref=send.at[to_inp * 16 + to_chan, tiles],
            dst_ref=got.at[me, tiles],
            send_sem=send_sem,
            recv_sem=recv_sem,
            device_id=(to_inp, to_chan),
            device_id_type=pl.DeviceIdType.MESH,
        ).start()
        return carry

    lax.fori_loop(1, 128, step, 0)
    local = pltpu.make_async_copy(send.at[me, tiles], got.at[me, tiles], local_sem)
    local.start()
    return local


def all_copies(send, got, tiles, send_sem, recv_sem):
    return pltpu.make_async_remote_copy(
        src_ref=send.at[pl.ds(0, 127), tiles],
        dst_ref=got.at[pl.ds(0, 127), tiles],
        send_sem=send_sem,
        recv_sem=recv_sem,
        device_id=(lax.axis_index("inp"), lax.axis_index("chan")),
        device_id_type=pl.DeviceIdType.MESH,
    )


def spectra_kernel(
    own_hbm, taper, high_hbm, low_hbm, history_hbm, matrix_hbm,
    own, history, left_send, right_send, left, right, high, low, rows, filtered, turned, gathered,
    sends, gots, matrix, load_sems, table_sems, halo_send_sems, halo_recv_sems, local_sems, send_sems, recv_sems, out_sems,
):
    inp, chan, device = place()
    chans = lax.axis_size("chan")
    first, last = chan == 0, chan == chans - 1
    width = FRAME // PIECES

    def loads(group, piece):
        inputs, lanes = pl.ds(16 * group, 16), pl.ds(width * piece, width)
        return pltpu.make_async_copy(own_hbm.at[inputs, :, lanes], own.at[inputs, :, lanes], load_sems.at[group, piece])

    tables = [
        pltpu.make_async_copy(high_hbm, high, table_sems.at[0]),
        pltpu.make_async_copy(low_hbm, low, table_sems.at[1]),
        pltpu.make_async_copy(history_hbm, history, table_sems.at[2]),
    ]
    for group in range(2):
        for piece in range(PIECES):
            loads(group, piece).start()
    for copy in tables:
        copy.start()

    barrier = pltpu.get_barrier_semaphore()

    def greet(n, carry):
        pl.semaphore_signal(barrier, inc=1, device_id=device(n), device_id_type=pl.DeviceIdType.MESH)
        return carry

    lax.fori_loop(1, 128, greet, 0)

    def halo_copies(group, piece):
        inputs, lanes = pl.ds(16 * group, 16), pl.ds(width * piece, width)
        return [
            pltpu.make_async_remote_copy(
                src_ref=source.at[pl.ds(0, count), inputs, lanes],
                dst_ref=target.at[pl.ds(0, count), inputs, lanes],
                send_sem=halo_send_sems.at[n, group, piece],
                recv_sem=halo_recv_sems.at[n, group, piece],
                device_id=(inp, (chan + by) % chans),
                device_id_type=pl.DeviceIdType.MESH,
            )
            for n, (source, target, by, count) in enumerate(
                ((left_send, left, 1, 4 - group), (right_send, right, chans - 1, 3 + group))
            )
        ]

    def column(group, col, slot):
        base = slot * 16 * STRIDE
        lanes = pl.ds(pl.multiple_of(col * LANES, LANES), LANES)
        for i in range(16):
            rows[pl.ds(base + i * STRIDE, 16), :] = own[group * 16 + i, :, lanes].astype(jnp.float32)

    def fir(edges, group, col, slot):
        base = slot * 16 * STRIDE
        lanes = pl.ds(pl.multiple_of(col * LANES, LANES), LANES)
        taps = taper[:, lanes]
        taps = [jnp.broadcast_to(taps[t : t + 1], (8, LANES)) for t in range(TAPS)]
        inputs = pl.ds(pl.multiple_of(group * 16, 16), 16)
        near = [rows[pl.ds(base + f, 16, stride=STRIDE), :] for f in range(16)]
        earlier, later = 4 - group, 3 + group
        if edges:
            past = [history[f, inputs, lanes].astype(jnp.float32) for f in range(7)]
            before = [left[f, inputs, lanes].astype(jnp.float32) for f in range(earlier)]
            before = [jnp.where(first, past[7 - earlier + f], before[f]) for f in range(earlier)]
            after = [right[f, inputs, lanes].astype(jnp.float32) for f in range(later)]
            start = before + near[:7]
            end = [jnp.where(last, past[f], near[9 + f]) for f in range(7)] + after
            windows = [start[o : o + TAPS] for o in range(earlier)] + [near[8:]]
            windows += [end[o : o + TAPS] for o in range(3)]
            if group == 1:
                windows = [end[3:]] + windows
        else:
            for n in range(earlier):
                left_send[n, inputs, lanes] = near[SPECTRA - earlier + n].astype(jnp.bfloat16)
            for n in range(later):
                right_send[n, inputs, lanes] = near[n].astype(jnp.bfloat16)
            windows = [near[o : o + TAPS] for o in range(8)]
        for h in range(2):
            for o, window in enumerate(windows):
                total = window[0][8 * h : 8 * h + 8] * taps[0]
                for t in range(1, TAPS):
                    total = total + window[t][8 * h : 8 * h + 8] * taps[t]
                filtered[o, col, pl.ds(8 * h, 8), :] = total

    def half(edges):
        for group in range(2):
            def columns(step, carry):
                for slot in range(SLOTS):
                    column(group, step * SLOTS + slot, slot)
                for slot in range(SLOTS):
                    fir(edges, group, step * SLOTS + slot, slot)
                return carry

            for piece in range(PIECES):
                if edges:
                    for copy in halo_copies(group, piece):
                        copy.wait()
                else:
                    loads(group, piece).wait()
                steps = COLS // SLOTS // PIECES
                lax.fori_loop(piece * steps, (piece + 1) * steps, columns, 0)
                if not edges:
                    if group == 0 and piece == 0:
                        pl.semaphore_wait(barrier, 127)
                    for copy in halo_copies(group, piece):
                        copy.start()

            def first_stage(o, carry):
                for part in range(2):
                    for h in range(2):
                        values = [filtered[o, 2 * a + part, pl.ds(8 * h, 8), :] for a in range(RADIX)]
                        re, im = real_fft(values)
                        im[0] = re[RADIX // 2]
                        row = pl.ds(pl.multiple_of(o * NIN + group * 16 + 8 * h, 8), 8)
                        for k in range(RADIX // 2):
                            turned[2 * k, row, part * LANES : (part + 1) * LANES] = re[k]
                            turned[2 * k + 1, row, part * LANES : (part + 1) * LANES] = im[k]
                return carry

            lax.fori_loop(0, 8, first_stage, 0)

        if not edges:
            for copy in tables:
                copy.wait()

        def second_stage(k, carry):
            both = jnp.concatenate([turned[2 * k], turned[2 * k + 1]], axis=1)
            both_high = both.astype(jnp.bfloat16)
            both_low = (both - both_high.astype(jnp.float32)).astype(jnp.bfloat16)

            def product(table, value):
                return lax.dot_general(table, value, (((1,), (1,)), ((), ())), preferred_element_type=jnp.float32)

            result = product(high[k], both_high) + product(high[k], both_low) + product(low[k], both_high)
            other = lax.rem(RADIX // 2 - k, RADIX // 2)
            for block in range(4):
                begin = 32 * (block // 2) + 16 * (block % 2) + (other if block >= 2 else k)
                for tile in range(2):
                    gathered[tile, pl.ds(begin, 64, stride=GAP), :] = result[
                        64 * block : 64 * block + 64, tile * LANES : (tile + 1) * LANES
                    ]
            return carry

        lax.fori_loop(0, RADIX // 2, second_stage, 0, unroll=4)

    def emit(send, tile):
        def step(block, carry):
            begin = pl.multiple_of(block * 8 * GAP, 8)
            for h in range(8):
                value = gathered[tile, pl.ds(begin + h * GAP, 64), :].astype(jnp.bfloat16)
                send[pl.ds(block * 16 + 2 * h, 2), tile] = value.reshape(2, 32, LANES)
            return carry

        lax.fori_loop(0, 8, step, 0)

    chunks = [(0, pl.ds(0, 2)), (1, pl.ds(0, 1)), (1, pl.ds(1, 1))]
    local_copies = []
    half(False)
    for n, (which, tiles) in enumerate(chunks):
        if n == 1:
            half(True)
        for tile in range(tiles.start, tiles.start + tiles.size):
            emit(sends.at[which], tile)
        local_copies.append(
            exchange(sends.at[which], gots.at[which], tiles, local_sems.at[n], send_sems.at[n], recv_sems.at[n])
        )
    writes = []
    for n, (which, tiles) in enumerate(chunks):
        all_copies(sends.at[which], gots.at[which], tiles, send_sems.at[n], recv_sems.at[n]).wait_recv()
        local_copies[n].wait()
        begin = 128 * which + 64 * tiles.start
        for tile in range(tiles.start, tiles.start + tiles.size):
            regroup(gots.at[which], rows, matrix, tile, 128 * which + 64 * tile, (which, tile) == (1, 0))
        block = (slice(None), slice(None), pl.ds(begin, 64 * tiles.size))
        writes.append(pltpu.make_async_copy(matrix.at[block], matrix_hbm.at[block], out_sems.at[n]))
        writes[-1].start()
    for n, (which, tiles) in enumerate(chunks):
        all_copies(sends.at[which], gots.at[which], tiles, send_sems.at[n], recv_sems.at[n]).wait_send()
        writes[n].wait()


def spectra(voltages, taper, high, low, history):
    any_space = pl.BlockSpec(memory_space=pl.ANY)
    vmem = pl.BlockSpec(memory_space=pltpu.VMEM)
    dma = pltpu.SemaphoreType.DMA
    return pl.pallas_call(
        spectra_kernel,
        out_shape=jax.ShapeDtypeStruct((16, 2, 256, 256), jnp.bfloat16),
        in_specs=[any_space, vmem, any_space, any_space, any_space],
        out_specs=any_space,
        scratch_shapes=[
            pltpu.VMEM((NIN, SPECTRA, FRAME), jnp.bfloat16),
            pltpu.VMEM((7, NIN, FRAME), jnp.bfloat16),
            *[pltpu.VMEM((4, NIN, FRAME), jnp.bfloat16) for _ in range(4)],
            pltpu.VMEM((16, 256, 512), jnp.bfloat16),
            pltpu.VMEM((16, 256, 512), jnp.bfloat16),
            pltpu.VMEM((SLOTS * 16 * STRIDE, LANES), jnp.float32),
            pltpu.VMEM((8, COLS, 16, LANES), jnp.float32),
            pltpu.VMEM((RADIX, 256, 256), jnp.float32),
            pltpu.VMEM((2, 64 * GAP, LANES), jnp.float32),
            pltpu.VMEM((2, 128, 2, 32, LANES), jnp.bfloat16),
            pltpu.VMEM((2, 128, 2, 32, LANES), jnp.bfloat16),
            pltpu.VMEM((16, 2, 256, 256), jnp.bfloat16),
            dma((2, PIECES)),
            dma((3,)),
            dma((2, 2, PIECES)),
            dma((2, 2, PIECES)),
            dma((3,)),
            dma((3,)),
            dma((3,)),
            dma((3,)),
        ],
        compiler_params=pltpu.CompilerParams(vmem_limit_bytes=60 << 20, has_side_effects=True, collective_id=0),
        cost_estimate=pl.CostEstimate(flops=30_000_000_000, bytes_accessed=25_000_000, transcendentals=0),
        name="spectra",
    )(voltages, taper, high, low, history)


def correlate_kernel(matrix, out):
    def product(left, right):
        return lax.dot_general(left, right, (((1,), (0,)), ((), ())), preferred_element_type=jnp.float32)

    scale = 1.0 / 256.0
    for n in range(out.shape[1]):
        re, im = matrix[n, 0], matrix[n, 1]
        re_t, im_t = re.T, im.T
        out[0, n] = ((product(re_t, re) + product(im_t, im)) * scale).astype(jnp.bfloat16)
        out[1, n] = ((product(im_t, re) - product(re_t, im)) * scale).astype(jnp.bfloat16)


def correlate(matrix):
    return pl.pallas_call(
        correlate_kernel,
        grid=(2,),
        out_shape=jax.ShapeDtypeStruct((2, 16, 256, 256), jnp.bfloat16),
        in_specs=[pl.BlockSpec((8, 2, 256, 256), lambda c: (c, 0, 0, 0))],
        out_specs=pl.BlockSpec((2, 8, 256, 256), lambda c: (0, c, 0, 0)),
        compiler_params=pltpu.CompilerParams(vmem_limit_bytes=60 << 20),
        cost_estimate=pl.CostEstimate(flops=4_300_000_000, bytes_accessed=9_000_000, transcendentals=0),
        name="correlate",
    )(matrix)


def on_device(voltages, history, taper):
    high, low = (jnp.asarray(t) for t in second_stage_tables())
    return correlate(spectra(voltages, taper, high, low, jnp.transpose(history, (1, 0, 2))))


def solution(mesh):
    in_specs = (P("inp", "chan", None), P("inp", None, None), P())
    out_specs = P(None, ("inp", "chan"), None, None)
    return jax.shard_map(on_device, mesh=mesh, in_specs=in_specs, out_specs=out_specs, check_vma=False)
```

```python
import functools
import math

import jax
import jax.numpy as jnp
import ml_dtypes
import numpy as np
from jax import lax
from jax.experimental import pallas as pl
from jax.experimental.pallas import tpu as pltpu
from jax.sharding import PartitionSpec as P

FRAME = 8192
LOW = 1024
BAND = 2048
TAPS = 8
RADIX = 32
INNER = FRAME // RADIX
LANES = 128
NIN = 32
SPECTRA = 16
STRIDE = 17
GAP = 65

COLS = FRAME // LANES
SLOTS = 4
PIECES = 4


def second_stage_tables():
    m = np.arange(INNER, dtype=np.int64)
    k1 = LOW // RADIX + np.arange(BAND // RADIX, dtype=np.int64)

    def angles(k0):
        index = (m[None, :] * (k0 + RADIX * k1[:, None])) % FRAME
        angle = index * (2.0 * math.pi / FRAME)
        return np.cos(angle), np.sin(angle)

    table = np.zeros((RADIX // 2, 4, k1.size, 2, INNER))
    for k0 in range(1, RADIX // 2):
        cos, sin = angles(k0)
        table[k0, 0, :, 0], table[k0, 0, :, 1] = cos, sin
        table[k0, 1, :, 0], table[k0, 1, :, 1] = -sin, cos
        cos, sin = angles(RADIX - k0)
        table[k0, 2, :, 0], table[k0, 2, :, 1] = cos, -sin
        table[k0, 3, :, 0], table[k0, 3, :, 1] = -sin, -cos
    cos, sin = angles(0)
    table[0, 0, :, 0], table[0, 1, :, 0] = cos, -sin
    cos, sin = angles(RADIX // 2)
    table[0, 2, :, 1], table[0, 3, :, 1] = cos, -sin
    table = (table / math.sqrt(FRAME)).reshape(RADIX // 2, 4 * k1.size, 2 * INNER)
    table = table.astype(np.float32)
    high = table.astype(ml_dtypes.bfloat16)
    low = (table - high.astype(np.float32)).astype(ml_dtypes.bfloat16)
    return high, low


def real_fft(values):
    n = len(values)
    if n == 2:
        return [values[0] + values[1], values[0] - values[1]], [None, None]
    even_re, even_im = real_fft(values[0::2])
    odd_re, odd_im = real_fft(values[1::2])
    re, im = [None] * (n // 2 + 1), [None] * (n // 2 + 1)
    re[0], re[n // 2] = even_re[0] + odd_re[0], even_re[0] - odd_re[0]
    re[n // 4], im[n // 4] = even_re[n // 4], -odd_re[n // 4]
    for k in range(1, n // 4):
        cos, sin = math.cos(2 * math.pi * k / n), math.sin(2 * math.pi * k / n)
        if 8 * k == n:
            turned_re = (odd_re[k] + odd_im[k]) * cos
            turned_im = (odd_im[k] - odd_re[k]) * cos
        else:
            turned_re = odd_re[k] * cos + odd_im[k] * sin
            turned_im = odd_im[k] * cos - odd_re[k] * sin
        re[k], im[k] = even_re[k] + turned_re, even_im[k] + turned_im
        re[n // 2 - k], im[n // 2 - k] = even_re[k] - turned_re, turned_im - even_im[k]
    return re, im


def regroup(ref, rows, matrix, tile, offset, turn):
    lane = lax.broadcasted_iota(jnp.int32, (16, LANES), 1)
    lower = lane < 64
    even = lane % 64 < 32
    ahead = lane % 32 >= 16

    def step(index, carry):
        part, quad = index // 2, index % 2
        for a in range(4):
            for src in range(16):
                value = ref[(quad * 4 + a) * 16 + src, tile, pl.ds(pl.multiple_of(part * 16, 16), 16), :]
                rows[pl.ds((a * 16 + src) * STRIDE, 16), :] = value.astype(jnp.float32)
        for c in range(16):
            t = [rows[pl.ds(a * 16 * STRIDE + c, 16, stride=STRIDE), :] for a in range(4)]
            u = [None] * 4
            for a in range(2):
                u[a] = jnp.where(lower, t[a], pltpu.roll(t[a + 2], 64, 1))
                u[a + 2] = jnp.where(lower, pltpu.roll(t[a], 64, 1), t[a + 2])
            for a in (0, 2):
                first = jnp.where(even, u[a], pltpu.roll(u[a + 1], 32, 1))
                second = jnp.where(even, pltpu.roll(u[a], 96, 1), u[a + 1])
                if turn and a == 0:
                    first = jnp.where(ahead, pltpu.roll(first, 1, 0), first)
                for b, value in enumerate((first, second)):
                    lanes = pl.ds(pl.multiple_of(quad * LANES, LANES), LANES)
                    matrix[c, part, pl.ds(offset + (a + b) * 16, 16), lanes] = value.astype(jnp.bfloat16)
        return carry

    lax.fori_loop(0, 4, step, 0)


def place():
    inp, chan = lax.axis_index("inp"), lax.axis_index("chan")
    rem, div = lax.rem, lax.div
    x, y, z, core = chan // 2 % 4, inp % 4, chan // 8 * 2 + inp // 4, chan % 2

    def device(n):
        n = rem(n * 27, 128)
        to_x, to_y, to_z = rem(x + div(n, 2), 4), rem(y + div(n, 8), 4), rem(z + div(n, 32), 4)
        return rem(to_z, 2) * 4 + to_y, div(to_z, 2) * 8 + to_x * 2 + rem(core + n, 2)

    return inp, chan, device


def exchange(send, got, tiles, local_sem, send_sem, recv_sem):
    inp, chan, device = place()
    me = inp * 16 + chan

    def step(n, carry):
        to_inp, to_chan = device(n)
        pltpu.make_async_remote_copy(
            src_ref=send.at[to_inp * 16 + to_chan, tiles],
            dst_ref=got.at[me, tiles],
            send_sem=send_sem,
            recv_sem=recv_sem,
            device_id=(to_inp, to_chan),
            device_id_type=pl.DeviceIdType.MESH,
        ).start()
        return carry

    lax.fori_loop(1, 128, step, 0)
    local = pltpu.make_async_copy(send.at[me, tiles], got.at[me, tiles], local_sem)
    local.start()
    return local


def all_copies(send, got, tiles, send_sem, recv_sem):
    return pltpu.make_async_remote_copy(
        src_ref=send.at[pl.ds(0, 127), tiles],
        dst_ref=got.at[pl.ds(0, 127), tiles],
        send_sem=send_sem,
        recv_sem=recv_sem,
        device_id=(lax.axis_index("inp"), lax.axis_index("chan")),
        device_id_type=pl.DeviceIdType.MESH,
    )


def spectra_kernel(
    own_hbm, taper, high_hbm, low_hbm, history_hbm, matrix_hbm,
    own, history, left_send, right_send, left, right, high, low, rows, filtered, turned, gathered,
    sends, gots, matrix, load_sems, table_sems, halo_send_sems, halo_recv_sems, local_sems, send_sems, recv_sems, out_sems,
):
    inp, chan, _ = place()
    chans = lax.axis_size("chan")
    first, last = chan == 0, chan == chans - 1
    width = FRAME // PIECES

    def loads(group, piece):
        inputs, lanes = pl.ds(16 * group, 16), pl.ds(width * piece, width)
        return pltpu.make_async_copy(own_hbm.at[inputs, :, lanes], own.at[inputs, :, lanes], load_sems.at[group, piece])

    tables = [
        pltpu.make_async_copy(high_hbm, high, table_sems.at[0]),
        pltpu.make_async_copy(low_hbm, low, table_sems.at[1]),
        pltpu.make_async_copy(history_hbm, history, table_sems.at[2]),
    ]
    for group in range(2):
        for piece in range(PIECES):
            loads(group, piece).start()
    for copy in tables:
        copy.start()

    barrier = pltpu.get_barrier_semaphore()

    inps = [lax.rem(inp + n, lax.axis_size("inp")) for n in range(lax.axis_size("inp"))]
    chan_list = [lax.rem(chan + n, chans) for n in range(chans)]
    for n in range(1, 128):
        there = (inps[n // chans], chan_list[n % chans])
        pl.semaphore_signal(barrier, inc=1, device_id=there, device_id_type=pl.DeviceIdType.MESH)

    def halo_copies(group, piece):
        inputs, lanes = pl.ds(16 * group, 16), pl.ds(width * piece, width)
        return [
            pltpu.make_async_remote_copy(
                src_ref=source.at[pl.ds(0, count), inputs, lanes],
                dst_ref=target.at[pl.ds(0, count), inputs, lanes],
                send_sem=halo_send_sems.at[n, group, piece],
                recv_sem=halo_recv_sems.at[n, group, piece],
                device_id=(inp, (chan + by) % chans),
                device_id_type=pl.DeviceIdType.MESH,
            )
            for n, (source, target, by, count) in enumerate(
                ((left_send, left, 1, 4 - group), (right_send, right, chans - 1, 3 + group))
            )
        ]

    def column(group, col, slot):
        base = slot * 16 * STRIDE
        lanes = pl.ds(pl.multiple_of(col * LANES, LANES), LANES)
        for i in range(16):
            rows[pl.ds(base + i * STRIDE, 16), :] = own[group * 16 + i, :, lanes].astype(jnp.float32)

    def fir(edges, group, col, slot):
        base = slot * 16 * STRIDE
        lanes = pl.ds(pl.multiple_of(col * LANES, LANES), LANES)
        taps = taper[:, lanes]
        taps = [jnp.broadcast_to(taps[t : t + 1], (8, LANES)) for t in range(TAPS)]
        inputs = pl.ds(pl.multiple_of(group * 16, 16), 16)
        near = [rows[pl.ds(base + f, 16, stride=STRIDE), :] for f in range(16)]
        earlier, later = 4 - group, 3 + group
        if edges:
            past = [history[f, inputs, lanes].astype(jnp.float32) for f in range(7)]
            before = [left[f, inputs, lanes].astype(jnp.float32) for f in range(earlier)]
            before = [jnp.where(first, past[7 - earlier + f], before[f]) for f in range(earlier)]
            after = [right[f, inputs, lanes].astype(jnp.float32) for f in range(later)]
            start = before + near[:7]
            end = [jnp.where(last, past[f], near[9 + f]) for f in range(7)] + after
            windows = [start[o : o + TAPS] for o in range(earlier)] + [near[8:]]
            windows += [end[o : o + TAPS] for o in range(3)]
            if group == 1:
                windows = [end[3:]] + windows
        else:
            for n in range(earlier):
                left_send[n, inputs, lanes] = near[SPECTRA - earlier + n].astype(jnp.bfloat16)
            for n in range(later):
                right_send[n, inputs, lanes] = near[n].astype(jnp.bfloat16)
            windows = [near[o : o + TAPS] for o in range(8)]
        for h in range(2):
            for o, window in enumerate(windows):
                total = window[0][8 * h : 8 * h + 8] * taps[0]
                for t in range(1, TAPS):
                    total = total + window[t][8 * h : 8 * h + 8] * taps[t]
                filtered[o, col, pl.ds(8 * h, 8), :] = total

    def half(edges):
        for group in range(2):
            def columns(step, carry):
                for slot in range(SLOTS):
                    column(group, step * SLOTS + slot, slot)
                for slot in range(SLOTS):
                    fir(edges, group, step * SLOTS + slot, slot)
                return carry

            for piece in range(PIECES):
                if edges:
                    for copy in halo_copies(group, piece):
                        copy.wait()
                else:
                    loads(group, piece).wait()
                steps = COLS // SLOTS // PIECES
                lax.fori_loop(piece * steps, (piece + 1) * steps, columns, 0)
                if not edges:
                    if group == 0 and piece == 0:
                        pl.semaphore_wait(barrier, 127)
                    for copy in halo_copies(group, piece):
                        copy.start()

            def first_stage(o, carry):
                for part in range(2):
                    for h in range(2):
                        values = [filtered[o, 2 * a + part, pl.ds(8 * h, 8), :] for a in range(RADIX)]
                        re, im = real_fft(values)
                        im[0] = re[RADIX // 2]
                        row = pl.ds(pl.multiple_of(o * NIN + group * 16 + 8 * h, 8), 8)
                        for k in range(RADIX // 2):
                            turned[2 * k, row, part * LANES : (part + 1) * LANES] = re[k]
                            turned[2 * k + 1, row, part * LANES : (part + 1) * LANES] = im[k]
                return carry

            lax.fori_loop(0, 8, first_stage, 0)

        if not edges:
            for copy in tables:
                copy.wait()

        def second_stage(k, carry):
            both = jnp.concatenate([turned[2 * k], turned[2 * k + 1]], axis=1)
            both_high = both.astype(jnp.bfloat16)
            both_low = (both - both_high.astype(jnp.float32)).astype(jnp.bfloat16)

            def product(table, value):
                return lax.dot_general(table, value, (((1,), (1,)), ((), ())), preferred_element_type=jnp.float32)

            result = product(high[k], both_high) + product(high[k], both_low) + product(low[k], both_high)
            other = lax.rem(RADIX // 2 - k, RADIX // 2)
            for block in range(4):
                begin = 32 * (block // 2) + 16 * (block % 2) + (other if block >= 2 else k)
                for tile in range(2):
                    gathered[tile, pl.ds(begin, 64, stride=GAP), :] = result[
                        64 * block : 64 * block + 64, tile * LANES : (tile + 1) * LANES
                    ]
            return carry

        lax.fori_loop(0, RADIX // 2, second_stage, 0, unroll=4)

    def emit(send, tile):
        def step(block, carry):
            begin = pl.multiple_of(block * 8 * GAP, 8)
            for h in range(8):
                value = gathered[tile, pl.ds(begin + h * GAP, 64), :].astype(jnp.bfloat16)
                send[pl.ds(block * 16 + 2 * h, 2), tile] = value.reshape(2, 32, LANES)
            return carry

        lax.fori_loop(0, 8, step, 0)

    chunks = [(0, pl.ds(0, 2)), (1, pl.ds(0, 1)), (1, pl.ds(1, 1))]
    local_copies = []
    half(False)
    for n, (which, tiles) in enumerate(chunks):
        if n == 1:
            half(True)
        for tile in range(tiles.start, tiles.start + tiles.size):
            emit(sends.at[which], tile)
        local_copies.append(
            exchange(sends.at[which], gots.at[which], tiles, local_sems.at[n], send_sems.at[n], recv_sems.at[n])
        )
    writes = []
    for n, (which, tiles) in enumerate(chunks):
        all_copies(sends.at[which], gots.at[which], tiles, send_sems.at[n], recv_sems.at[n]).wait_recv()
        local_copies[n].wait()
        begin = 128 * which + 64 * tiles.start
        for tile in range(tiles.start, tiles.start + tiles.size):
            regroup(gots.at[which], rows, matrix, tile, 128 * which + 64 * tile, (which, tile) == (1, 0))
        block = (slice(None), slice(None), pl.ds(begin, 64 * tiles.size))
        writes.append(pltpu.make_async_copy(matrix.at[block], matrix_hbm.at[block], out_sems.at[n]))
        writes[-1].start()
    for n, (which, tiles) in enumerate(chunks):
        all_copies(sends.at[which], gots.at[which], tiles, send_sems.at[n], recv_sems.at[n]).wait_send()
        writes[n].wait()


def spectra(voltages, taper, high, low, history):
    any_space = pl.BlockSpec(memory_space=pl.ANY)
    vmem = pl.BlockSpec(memory_space=pltpu.VMEM)
    dma = pltpu.SemaphoreType.DMA
    return pl.pallas_call(
        spectra_kernel,
        out_shape=jax.ShapeDtypeStruct((16, 2, 256, 256), jnp.bfloat16),
        in_specs=[any_space, vmem, any_space, any_space, any_space],
        out_specs=any_space,
        scratch_shapes=[
            pltpu.VMEM((NIN, SPECTRA, FRAME), jnp.bfloat16),
            pltpu.VMEM((7, NIN, FRAME), jnp.bfloat16),
            *[pltpu.VMEM((4, NIN, FRAME), jnp.bfloat16) for _ in range(4)],
            pltpu.VMEM((16, 256, 512), jnp.bfloat16),
            pltpu.VMEM((16, 256, 512), jnp.bfloat16),
            pltpu.VMEM((SLOTS * 16 * STRIDE, LANES), jnp.float32),
            pltpu.VMEM((8, COLS, 16, LANES), jnp.float32),
            pltpu.VMEM((RADIX, 256, 256), jnp.float32),
            pltpu.VMEM((2, 64 * GAP, LANES), jnp.float32),
            pltpu.VMEM((2, 128, 2, 32, LANES), jnp.bfloat16),
            pltpu.VMEM((2, 128, 2, 32, LANES), jnp.bfloat16),
            pltpu.VMEM((16, 2, 256, 256), jnp.bfloat16),
            dma((2, PIECES)),
            dma((3,)),
            dma((2, 2, PIECES)),
            dma((2, 2, PIECES)),
            dma((3,)),
            dma((3,)),
            dma((3,)),
            dma((3,)),
        ],
        compiler_params=pltpu.CompilerParams(vmem_limit_bytes=60 << 20, has_side_effects=True, collective_id=0),
        cost_estimate=pl.CostEstimate(flops=30_000_000_000, bytes_accessed=25_000_000, transcendentals=0),
        name="spectra",
    )(voltages, taper, high, low, history)


def correlate_kernel(matrix, out):
    def product(left, right):
        return lax.dot_general(left, right, (((1,), (0,)), ((), ())), preferred_element_type=jnp.float32)

    scale = 1.0 / 256.0
    for n in range(out.shape[1]):
        re, im = matrix[n, 0], matrix[n, 1]
        re_t, im_t = re.T, im.T
        out[0, n] = ((product(re_t, re) + product(im_t, im)) * scale).astype(jnp.bfloat16)
        out[1, n] = ((product(im_t, re) - product(re_t, im)) * scale).astype(jnp.bfloat16)


def correlate(matrix):
    return pl.pallas_call(
        correlate_kernel,
        grid=(2,),
        out_shape=jax.ShapeDtypeStruct((2, 16, 256, 256), jnp.bfloat16),
        in_specs=[pl.BlockSpec((8, 2, 256, 256), lambda c: (c, 0, 0, 0))],
        out_specs=pl.BlockSpec((2, 8, 256, 256), lambda c: (0, c, 0, 0)),
        compiler_params=pltpu.CompilerParams(vmem_limit_bytes=60 << 20),
        cost_estimate=pl.CostEstimate(flops=4_300_000_000, bytes_accessed=9_000_000, transcendentals=0),
        name="correlate",
    )(matrix)


def on_device(voltages, history, taper):
    high, low = (jnp.asarray(t) for t in second_stage_tables())
    return correlate(spectra(voltages, taper, high, low, jnp.transpose(history, (1, 0, 2))))


def solution(mesh):
    in_specs = (P("inp", "chan", None), P("inp", None, None), P())
    out_specs = P(None, ("inp", "chan"), None, None)
    return jax.shard_map(on_device, mesh=mesh, in_specs=in_specs, out_specs=out_specs, check_vma=False)
```

```python
import functools
import math

import jax
import jax.numpy as jnp
import ml_dtypes
import numpy as np
from jax import lax
from jax.experimental import pallas as pl
from jax.experimental.pallas import tpu as pltpu
from jax.sharding import PartitionSpec as P

FRAME = 8192
LOW = 1024
BAND = 2048
TAPS = 8
RADIX = 32
INNER = FRAME // RADIX
LANES = 128
NIN = 32
SPECTRA = 16
STRIDE = 17
GAP = 65

COLS = FRAME // LANES
SLOTS = 4
PIECES = 4


def second_stage_tables():
    m = np.arange(INNER, dtype=np.int64)
    k1 = LOW // RADIX + np.arange(BAND // RADIX, dtype=np.int64)

    def angles(k0):
        index = (m[None, :] * (k0 + RADIX * k1[:, None])) % FRAME
        angle = index * (2.0 * math.pi / FRAME)
        return np.cos(angle), np.sin(angle)

    table = np.zeros((RADIX // 2, 4, k1.size, 2, INNER))
    for k0 in range(1, RADIX // 2):
        cos, sin = angles(k0)
        table[k0, 0, :, 0], table[k0, 0, :, 1] = cos, sin
        table[k0, 1, :, 0], table[k0, 1, :, 1] = -sin, cos
        cos, sin = angles(RADIX - k0)
        table[k0, 2, :, 0], table[k0, 2, :, 1] = cos, -sin
        table[k0, 3, :, 0], table[k0, 3, :, 1] = -sin, -cos
    cos, sin = angles(0)
    table[0, 0, :, 0], table[0, 1, :, 0] = cos, -sin
    cos, sin = angles(RADIX // 2)
    table[0, 2, :, 1], table[0, 3, :, 1] = cos, -sin
    table = (table / math.sqrt(FRAME)).reshape(RADIX // 2, 4 * k1.size, 2 * INNER)
    table = table.astype(np.float32)
    high = table.astype(ml_dtypes.bfloat16)
    low = (table - high.astype(np.float32)).astype(ml_dtypes.bfloat16)
    return high, low


def real_fft(values):
    n = len(values)
    if n == 2:
        return [values[0] + values[1], values[0] - values[1]], [None, None]
    even_re, even_im = real_fft(values[0::2])
    odd_re, odd_im = real_fft(values[1::2])
    re, im = [None] * (n // 2 + 1), [None] * (n // 2 + 1)
    re[0], re[n // 2] = even_re[0] + odd_re[0], even_re[0] - odd_re[0]
    re[n // 4], im[n // 4] = even_re[n // 4], -odd_re[n // 4]
    for k in range(1, n // 4):
        cos, sin = math.cos(2 * math.pi * k / n), math.sin(2 * math.pi * k / n)
        if 8 * k == n:
            turned_re = (odd_re[k] + odd_im[k]) * cos
            turned_im = (odd_im[k] - odd_re[k]) * cos
        else:
            turned_re = odd_re[k] * cos + odd_im[k] * sin
            turned_im = odd_im[k] * cos - odd_re[k] * sin
        re[k], im[k] = even_re[k] + turned_re, even_im[k] + turned_im
        re[n // 2 - k], im[n // 2 - k] = even_re[k] - turned_re, turned_im - even_im[k]
    return re, im


def regroup(ref, rows, matrix, tile, offset, turn):
    lane = lax.broadcasted_iota(jnp.int32, (16, LANES), 1)
    lower = lane < 64
    even = lane % 64 < 32
    ahead = lane % 32 >= 16

    def step(index, carry):
        part, quad = index // 2, index % 2
        for a in range(4):
            for src in range(16):
                value = ref[(quad * 4 + a) * 16 + src, tile, pl.ds(pl.multiple_of(part * 16, 16), 16), :]
                rows[pl.ds((a * 16 + src) * STRIDE, 16), :] = value.astype(jnp.float32)
        for c in range(16):
            t = [rows[pl.ds(a * 16 * STRIDE + c, 16, stride=STRIDE), :] for a in range(4)]
            u = [None] * 4
            for a in range(2):
                u[a] = jnp.where(lower, t[a], pltpu.roll(t[a + 2], 64, 1))
                u[a + 2] = jnp.where(lower, pltpu.roll(t[a], 64, 1), t[a + 2])
            for a in (0, 2):
                first = jnp.where(even, u[a], pltpu.roll(u[a + 1], 32, 1))
                second = jnp.where(even, pltpu.roll(u[a], 96, 1), u[a + 1])
                if turn and a == 0:
                    first = jnp.where(ahead, pltpu.roll(first, 1, 0), first)
                for b, value in enumerate((first, second)):
                    lanes = pl.ds(pl.multiple_of(quad * LANES, LANES), LANES)
                    matrix[c, part, pl.ds(offset + (a + b) * 16, 16), lanes] = value.astype(jnp.bfloat16)
        return carry

    lax.fori_loop(0, 4, step, 0)


def place():
    inp, chan = lax.axis_index("inp"), lax.axis_index("chan")
    rem, div = lax.rem, lax.div
    x, y, z, core = rem(div(chan, 2), 4), rem(inp, 4), div(chan, 8) * 2 + div(inp, 4), rem(chan, 2)
    xs, ys, zs = ([rem(v + n, 4) for n in range(4)] for v in (x, y, z))
    highs, lows = [div(v, 2) * 8 for v in zs], [rem(v, 2) * 4 for v in zs]
    pairs = [[v * 2 + rem(core + n, 2) for n in range(2)] for v in xs]

    def device(n):
        n = n * 27 % 128
        return lows[n // 32] + ys[n // 8 % 4], highs[n // 32] + pairs[n // 2 % 4][n % 2]

    return inp, chan, device


def exchange(send, got, tiles, local_sem, send_sem, recv_sem):
    inp, chan, device = place()
    me = inp * 16 + chan

    for n in range(1, 128):
        to_inp, to_chan = device(n)
        pltpu.make_async_remote_copy(
            src_ref=send.at[to_inp * 16 + to_chan, tiles],
            dst_ref=got.at[me, tiles],
            send_sem=send_sem,
            recv_sem=recv_sem,
            device_id=(to_inp, to_chan),
            device_id_type=pl.DeviceIdType.MESH,
        ).start()
    local = pltpu.make_async_copy(send.at[me, tiles], got.at[me, tiles], local_sem)
    local.start()
    return local


def all_copies(send, got, tiles, send_sem, recv_sem):
    return pltpu.make_async_remote_copy(
        src_ref=send.at[pl.ds(0, 127), tiles],
        dst_ref=got.at[pl.ds(0, 127), tiles],
        send_sem=send_sem,
        recv_sem=recv_sem,
        device_id=(lax.axis_index("inp"), lax.axis_index("chan")),
        device_id_type=pl.DeviceIdType.MESH,
    )


def spectra_kernel(
    own_hbm, taper, high_hbm, low_hbm, history_hbm, matrix_hbm,
    own, history, left_send, right_send, left, right, high, low, rows, filtered, turned, gathered,
    sends, gots, matrix, load_sems, table_sems, halo_send_sems, halo_recv_sems, local_sems, send_sems, recv_sems, out_sems,
):
    inp, chan, _ = place()
    chans = lax.axis_size("chan")
    first, last = chan == 0, chan == chans - 1
    width = FRAME // PIECES

    def loads(group, piece):
        inputs, lanes = pl.ds(16 * group, 16), pl.ds(width * piece, width)
        return pltpu.make_async_copy(own_hbm.at[inputs, :, lanes], own.at[inputs, :, lanes], load_sems.at[group, piece])

    tables = [
        pltpu.make_async_copy(high_hbm, high, table_sems.at[0]),
        pltpu.make_async_copy(low_hbm, low, table_sems.at[1]),
        pltpu.make_async_copy(history_hbm, history, table_sems.at[2]),
    ]
    for piece in range(PIECES):
        loads(0, piece).start()

    barrier = pltpu.get_barrier_semaphore()

    inps = [lax.rem(inp + n, lax.axis_size("inp")) for n in range(lax.axis_size("inp"))]
    chan_list = [lax.rem(chan + n, chans) for n in range(chans)]
    for n in range(1, 128):
        there = (inps[n // chans], chan_list[n % chans])
        pl.semaphore_signal(barrier, inc=1, device_id=there, device_id_type=pl.DeviceIdType.MESH)

    def halo_copies(group, piece):
        inputs, lanes = pl.ds(16 * group, 16), pl.ds(width * piece, width)
        return [
            pltpu.make_async_remote_copy(
                src_ref=source.at[pl.ds(0, count), inputs, lanes],
                dst_ref=target.at[pl.ds(0, count), inputs, lanes],
                send_sem=halo_send_sems.at[n, group, piece],
                recv_sem=halo_recv_sems.at[n, group, piece],
                device_id=(inp, (chan + by) % chans),
                device_id_type=pl.DeviceIdType.MESH,
            )
            for n, (source, target, by, count) in enumerate(
                ((left_send, left, 1, 4 - group), (right_send, right, chans - 1, 3 + group))
            )
        ]

    def column(group, col, slot):
        base = slot * 16 * STRIDE
        lanes = pl.ds(pl.multiple_of(col * LANES, LANES), LANES)
        for i in range(16):
            rows[pl.ds(base + i * STRIDE, 16), :] = own[group * 16 + i, :, lanes].astype(jnp.float32)

    def fir(edges, group, col, slot):
        base = slot * 16 * STRIDE
        lanes = pl.ds(pl.multiple_of(col * LANES, LANES), LANES)
        taps = taper[:, lanes]
        taps = [jnp.broadcast_to(taps[t : t + 1], (8, LANES)) for t in range(TAPS)]
        inputs = pl.ds(pl.multiple_of(group * 16, 16), 16)
        near = [rows[pl.ds(base + f, 16, stride=STRIDE), :] for f in range(16)]
        earlier, later = 4 - group, 3 + group
        if edges:
            past = [history[f, inputs, lanes].astype(jnp.float32) for f in range(7)]
            before = [left[f, inputs, lanes].astype(jnp.float32) for f in range(earlier)]
            before = [jnp.where(first, past[7 - earlier + f], before[f]) for f in range(earlier)]
            after = [right[f, inputs, lanes].astype(jnp.float32) for f in range(later)]
            start = before + near[:7]
            end = [jnp.where(last, past[f], near[9 + f]) for f in range(7)] + after
            windows = [start[o : o + TAPS] for o in range(earlier)] + [near[8:]]
            windows += [end[o : o + TAPS] for o in range(3)]
            if group == 1:
                windows = [end[3:]] + windows
        else:
            for n in range(earlier):
                left_send[n, inputs, lanes] = near[SPECTRA - earlier + n].astype(jnp.bfloat16)
            for n in range(later):
                right_send[n, inputs, lanes] = near[n].astype(jnp.bfloat16)
            windows = [near[o : o + TAPS] for o in range(8)]
        for h in range(2):
            for o, window in enumerate(windows):
                total = window[0][8 * h : 8 * h + 8] * taps[0]
                for t in range(1, TAPS):
                    total = total + window[t][8 * h : 8 * h + 8] * taps[t]
                filtered[o, col, pl.ds(8 * h, 8), :] = total

    def half(edges):
        for group in range(2):
            def columns(step, carry):
                for slot in range(SLOTS):
                    column(group, step * SLOTS + slot, slot)
                for slot in range(SLOTS):
                    fir(edges, group, step * SLOTS + slot, slot)
                return carry

            for piece in range(PIECES):
                if edges:
                    for copy in halo_copies(group, piece):
                        copy.wait()
                else:
                    loads(group, piece).wait()
                    if group == 0:
                        loads(1, piece).start()
                    elif piece == 0:
                        for copy in tables:
                            copy.start()
                steps = COLS // SLOTS // PIECES
                lax.fori_loop(piece * steps, (piece + 1) * steps, columns, 0)
                if not edges:
                    if group == 0 and piece == 0:
                        pl.semaphore_wait(barrier, 127)
                    for copy in halo_copies(group, piece):
                        copy.start()

            def first_stage(o, carry):
                for part in range(2):
                    for h in range(2):
                        values = [filtered[o, 2 * a + part, pl.ds(8 * h, 8), :] for a in range(RADIX)]
                        re, im = real_fft(values)
                        im[0] = re[RADIX // 2]
                        row = pl.ds(pl.multiple_of(o * NIN + group * 16 + 8 * h, 8), 8)
                        for k in range(RADIX // 2):
                            turned[2 * k, row, part * LANES : (part + 1) * LANES] = re[k]
                            turned[2 * k + 1, row, part * LANES : (part + 1) * LANES] = im[k]
                return carry

            lax.fori_loop(0, 8, first_stage, 0)

        if not edges:
            for copy in tables:
                copy.wait()

        def second_stage(k, carry):
            both = jnp.concatenate([turned[2 * k], turned[2 * k + 1]], axis=1)
            both_high = both.astype(jnp.bfloat16)
            both_low = (both - both_high.astype(jnp.float32)).astype(jnp.bfloat16)

            def product(table, value):
                return lax.dot_general(table, value, (((1,), (1,)), ((), ())), preferred_element_type=jnp.float32)

            result = product(high[k], both_high) + product(high[k], both_low) + product(low[k], both_high)
            other = lax.rem(RADIX // 2 - k, RADIX // 2)
            for block in range(4):
                begin = 32 * (block // 2) + 16 * (block % 2) + (other if block >= 2 else k)
                for tile in range(2):
                    gathered[tile, pl.ds(begin, 64, stride=GAP), :] = result[
                        64 * block : 64 * block + 64, tile * LANES : (tile + 1) * LANES
                    ]
            return carry

        lax.fori_loop(0, RADIX // 2, second_stage, 0, unroll=4)

    def emit(send, tile):
        def step(block, carry):
            begin = pl.multiple_of(block * 8 * GAP, 8)
            for h in range(8):
                value = gathered[tile, pl.ds(begin + h * GAP, 64), :].astype(jnp.bfloat16)
                send[pl.ds(block * 16 + 2 * h, 2), tile] = value.reshape(2, 32, LANES)
            return carry

        lax.fori_loop(0, 8, step, 0)

    chunks = [(0, pl.ds(0, 2)), (1, pl.ds(0, 1)), (1, pl.ds(1, 1))]
    local_copies = []
    half(False)
    for n, (which, tiles) in enumerate(chunks):
        if n == 1:
            half(True)
        for tile in range(tiles.start, tiles.start + tiles.size):
            emit(sends.at[which], tile)
        local_copies.append(
            exchange(sends.at[which], gots.at[which], tiles, local_sems.at[n], send_sems.at[n], recv_sems.at[n])
        )
    writes = []
    for n, (which, tiles) in enumerate(chunks):
        all_copies(sends.at[which], gots.at[which], tiles, send_sems.at[n], recv_sems.at[n]).wait_recv()
        local_copies[n].wait()
        begin = 128 * which + 64 * tiles.start
        for tile in range(tiles.start, tiles.start + tiles.size):
            regroup(gots.at[which], rows, matrix, tile, 128 * which + 64 * tile, (which, tile) == (1, 0))
        block = (slice(None), slice(None), pl.ds(begin, 64 * tiles.size))
        writes.append(pltpu.make_async_copy(matrix.at[block], matrix_hbm.at[block], out_sems.at[n]))
        writes[-1].start()
    for n, (which, tiles) in enumerate(chunks):
        all_copies(sends.at[which], gots.at[which], tiles, send_sems.at[n], recv_sems.at[n]).wait_send()
        writes[n].wait()


def spectra(voltages, taper, high, low, history):
    any_space = pl.BlockSpec(memory_space=pl.ANY)
    vmem = pl.BlockSpec(memory_space=pltpu.VMEM)
    dma = pltpu.SemaphoreType.DMA
    return pl.pallas_call(
        spectra_kernel,
        out_shape=jax.ShapeDtypeStruct((16, 2, 256, 256), jnp.bfloat16),
        in_specs=[any_space, vmem, any_space, any_space, any_space],
        out_specs=any_space,
        scratch_shapes=[
            pltpu.VMEM((NIN, SPECTRA, FRAME), jnp.bfloat16),
            pltpu.VMEM((7, NIN, FRAME), jnp.bfloat16),
            *[pltpu.VMEM((4, NIN, FRAME), jnp.bfloat16) for _ in range(4)],
            pltpu.VMEM((16, 256, 512), jnp.bfloat16),
            pltpu.VMEM((16, 256, 512), jnp.bfloat16),
            pltpu.VMEM((SLOTS * 16 * STRIDE, LANES), jnp.float32),
            pltpu.VMEM((8, COLS, 16, LANES), jnp.float32),
            pltpu.VMEM((RADIX, 256, 256), jnp.float32),
            pltpu.VMEM((2, 64 * GAP, LANES), jnp.float32),
            pltpu.VMEM((2, 128, 2, 32, LANES), jnp.bfloat16),
            pltpu.VMEM((2, 128, 2, 32, LANES), jnp.bfloat16),
            pltpu.VMEM((16, 2, 256, 256), jnp.bfloat16),
            dma((2, PIECES)),
            dma((3,)),
            dma((2, 2, PIECES)),
            dma((2, 2, PIECES)),
            dma((3,)),
            dma((3,)),
            dma((3,)),
            dma((3,)),
        ],
        compiler_params=pltpu.CompilerParams(vmem_limit_bytes=60 << 20, has_side_effects=True, collective_id=0),
        cost_estimate=pl.CostEstimate(flops=30_000_000_000, bytes_accessed=25_000_000, transcendentals=0),
        name="spectra",
    )(voltages, taper, high, low, history)


def correlate_kernel(matrix, out):
    def product(left, right):
        return lax.dot_general(left, right, (((1,), (0,)), ((), ())), preferred_element_type=jnp.float32)

    scale = 1.0 / 256.0
    for n in range(out.shape[1]):
        re, im = matrix[n, 0], matrix[n, 1]
        re_t, im_t = re.T, im.T
        out[0, n] = ((product(re_t, re) + product(im_t, im)) * scale).astype(jnp.bfloat16)
        out[1, n] = ((product(im_t, re) - product(re_t, im)) * scale).astype(jnp.bfloat16)


def correlate(matrix):
    return pl.pallas_call(
        correlate_kernel,
        grid=(2,),
        out_shape=jax.ShapeDtypeStruct((2, 16, 256, 256), jnp.bfloat16),
        in_specs=[pl.BlockSpec((8, 2, 256, 256), lambda c: (c, 0, 0, 0))],
        out_specs=pl.BlockSpec((2, 8, 256, 256), lambda c: (0, c, 0, 0)),
        compiler_params=pltpu.CompilerParams(vmem_limit_bytes=60 << 20),
        cost_estimate=pl.CostEstimate(flops=4_300_000_000, bytes_accessed=9_000_000, transcendentals=0),
        name="correlate",
    )(matrix)


def on_device(voltages, history, taper):
    high, low = (jnp.asarray(t) for t in second_stage_tables())
    return correlate(spectra(voltages, taper, high, low, jnp.transpose(history, (1, 0, 2))))


def solution(mesh):
    in_specs = (P("inp", "chan", None), P("inp", None, None), P())
    out_specs = P(None, ("inp", "chan"), None, None)
    return jax.shard_map(on_device, mesh=mesh, in_specs=in_specs, out_specs=out_specs, check_vma=False)
```
